32 devices in a mesh: seq: 8 (over z, x), chan: 4 (over y, core).
Axes of the slice: x: 2, y: 2, z: 4, core: 2. Of those that a mesh axis runs over, the one named last changes fastest.
Arguments:
- tokens: bfloat16 [2048, 8192], P('seq', 'chan'), may hold values from -700 to 700
- cotangent: bfloat16 [2048, 8192], P('seq', 'chan'), may hold values from -6 to 6
- filters: bfloat16 [256, 8192], P(None, 'chan'), may hold values from -0.375 to 0.375
- gain: float32 [8192], P('chan'), may hold values from 0.25 to 1.75
Outputs:
- conv_out: bfloat16 [2048, 8192], P('seq', 'chan')
- input_grad: bfloat16 [2048, 8192], P('seq', 'chan')
- filter_grad: float32 [256, 8192], P(None, 'chan')
- gain_grad: float32 [8192], P('chan')
The draws below stay inside these ranges and needn't reach their ends.
All inputs are finite; a program needn't handle non-finite values.
Results may differ from the reference program's by a relative error of at most 0.005.
Values may be sent and summed in bfloat16 or wider, within the bound.
A program may use at most 64 MiB of HBM per device.

```python
import math
import jax
import jax.numpy as jnp
from jax import lax

D = 8192
TOKENS = 2048
FLEN = 256


def draw_tokens(key, part):
    first, second, third = jax.random.split(jax.random.fold_in(key, 11), 3)
    column = jnp.arange(D, dtype=jnp.float32) / D
    col_scale = jnp.exp(math.log(10.0) * column) * jax.random.uniform(second, (D,), jnp.float32, 0.6, 1.4)
    row_scale = jnp.exp(math.log(10.0) * jax.random.uniform(third, (TOKENS, 1), jnp.float32))
    base = jnp.clip(jax.random.normal(first, (TOKENS, D), jnp.float32), -5.0, 5.0)
    return (base * row_scale * col_scale[None, :]).astype(jnp.bfloat16)


def shard_levels(own_key, shape, shards, smallest, top_value):
    factor_of, own = 1.0, jax.random.fold_in(own_key, 6)
    for axis_at, parts in shards:
        steps = jnp.exp(jax.random.uniform(jax.random.fold_in(own, axis_at), (parts,), jnp.float32, smallest / len(shards), top_value / len(shards)))
        factor_of = factor_of * jnp.repeat(steps, shape[axis_at] // parts).reshape([-1 if axis == axis_at else 1 for axis in range(len(shape))])
    return factor_of


def scatter_about(rng, extent, deviation, most, cuts=(), held_as=jnp.bfloat16):
    values = deviation * jax.random.normal(rng, extent, jnp.float32)
    if cuts:
        values = values * shard_levels(rng, extent, cuts, -0.22, 0.18)
    return jnp.clip(values, -most, most).astype(held_as)


def setup_inputs(seed: int = 0) -> dict:
    streams_of = jax.random.split(jax.random.key(seed), 5)
    return {
        "tokens": draw_tokens(jax.random.fold_in(streams_of[4], 71), 0),
        "cotangent": scatter_about(streams_of[1], (TOKENS, D), 1.0, 6.0, ((0, 8), (1, 4))),
        "filters": scatter_about(streams_of[2], (FLEN, D), FLEN ** -0.5, 0.375, ((1, 4),)),
        "gain": jnp.clip(1.0 + 0.15 * jax.random.normal(streams_of[3], (D,), jnp.float32), 0.25, 1.75),
    }


def group_grads(pieces):
    normed, gradient, taps, scaled = pieces
    length = 2 * TOKENS
    spec_in = jnp.fft.rfft(normed, n=length, axis=0)
    spec_taps = jnp.fft.rfft(taps, n=length, axis=0)
    spec_grad = jnp.fft.rfft(gradient, n=length, axis=0)
    conv_full = jnp.fft.irfft(spec_in * spec_taps, n=length, axis=0)[:TOKENS]
    upstream = jnp.fft.irfft(spec_grad * jnp.conj(spec_taps), n=length, axis=0)[:TOKENS]
    taps_grad = jnp.fft.irfft(spec_grad * jnp.conj(spec_in), n=length, axis=0)[:FLEN]
    gain_part = lax.optimization_barrier(jnp.sum(upstream * scaled, axis=0))
    return (conv_full, upstream, taps_grad, gain_part)

def reference(tokens, cotangent, filters, gain):
    values = tokens.astype(jnp.float32)
    factor = lax.rsqrt(lax.optimization_barrier(jnp.mean(values * values, axis=1, keepdims=True)) + 1e-06)
    rounded = (values * factor * gain).astype(jnp.bfloat16)
    rounded = lax.optimization_barrier(rounded)
    normed = rounded.astype(jnp.float32)
    group = math.gcd(D, 512)
    blocks = D // group

    def split_groups(array):
        return array.reshape(array.shape[0], blocks, group).transpose(1, 0, 2)

    def join_groups(array):
        return array.transpose(1, 0, 2).reshape(array.shape[1], D)
    conv_full, upstream, taps_grad, gain_part = lax.map(group_grads, (split_groups(normed), split_groups(cotangent.astype(jnp.float32)), split_groups(filters.astype(jnp.float32)), split_groups(values * factor)))
    norm_factor = 1.0 / math.sqrt(TOKENS)
    conv_out = join_groups(conv_full).astype(jnp.bfloat16)
    input_grad = join_groups(upstream).astype(jnp.bfloat16)
    filter_grad = join_groups(taps_grad) * norm_factor
    gain_grad = gain_part.reshape(D) * norm_factor
    return (conv_out, input_grad, filter_grad, gain_grad)
```

```python
import functools
import math

import jax
import jax.numpy as jnp
import ml_dtypes
import numpy as np
from jax import lax
from jax.experimental import pallas as pl
from jax.experimental.pallas import tpu as pltpu
from jax.sharding import PartitionSpec as P

MESH = pl.DeviceIdType.MESH
DEPTH = 3
DIRECT = 1


def halves(matrix):
    high = matrix.astype(ml_dtypes.bfloat16)
    low = (matrix - high.astype(np.float64)).astype(ml_dtypes.bfloat16)
    return high, low


def transforms(rows):
    odd = 2 * np.arange(rows)[:, None] + 1
    angle = np.pi / (2 * rows) * ((odd * np.arange(rows)[None, :]) % (4 * rows))
    forward = np.concatenate([np.cos(angle), -np.sin(angle)], axis=0)
    return (*halves(forward), *halves(forward.T / rows))


def kernel(
    sizes,
    tok, cot, fil, gain, fh, fl, ih, il,
    conv, igrad, fgrad, ggrad,
    nrm, htok, hcot, hop, ssq, fac, spec_h, spec_a, spec_g, part, below, acc, near, total, gsum,
    cot_s, cot_r, tok_s, tok_r, hop_s, hop_r, ssq_s, ssq_r, up_s, up_r, near_s, near_r, down_s, down_r, gs_s, gs_r,
):
    shards, groups, chunks, width, model_width, scale = sizes
    rows = tok.shape[0]
    half = rows // 2
    pairs = shards // 2
    me, my_chan = lax.axis_index("seq"), lax.axis_index("chan")
    side, level = lax.rem(me, 2), lax.div(me, 2)
    twin = me + 1 - 2 * side
    top = pairs - 1
    past, after = lax.rem(me + shards - 1, shards), lax.rem(me + 1, shards)
    above, under = lax.rem(me + 2, shards), lax.rem(me + shards - 2, shards)
    sign = (1 - 2 * (lax.broadcasted_iota(jnp.int32, (rows, width), 0) & 1)).astype(jnp.float32)

    def cols(k):
        return pl.ds(pl.multiple_of(k * width, width), width)

    def every(count, body, first=0):
        lax.fori_loop(first, count, lambda i, c: (body(i), c)[1], 0)

    def others(count, mine, body):
        def step(i):
            @pl.when(i != mine)
            def _():
                body(i)
        every(count, step)

    def remote(src, dst, ssem, rsem, seq, chan):
        return pltpu.make_async_remote_copy(
            src_ref=src, dst_ref=dst, send_sem=ssem, recv_sem=rsem, device_id=(seq, chan), device_id_type=MESH)

    def cot_copy(k):
        return remote(cot.at[:, cols(k)], hcot.at[k], cot_s.at[k], cot_r.at[k], past, my_chan)

    def tok_copy(k):
        return remote(nrm.at[k], htok.at[k], tok_s.at[k], tok_r.at[k], after, my_chan)

    def detour_copy(k):
        return remote(nrm.at[k], hop.at[k], tok_s.at[k], hop_r.at[k], twin, my_chan)

    def hop_copy(k):
        return remote(hop.at[k], htok.at[k], hop_s.at[k], tok_r.at[k], above, my_chan)

    def ssq_copy(to, at):
        return remote(ssq.at[at], ssq.at[at], ssq_s.at[to], ssq_r.at[at], me, to)

    def piece(h):
        return pl.ds(h * half, half)

    def up_copy(k, h):
        return remote(acc.at[k, piece(h)], below.at[k, piece(h)], up_s.at[k, h], up_r.at[k, h], above, my_chan)

    def near_copy(k, h):
        return remote(acc.at[k, piece(h)], near.at[k, piece(h)], near_s.at[k, h], near_r.at[k, h], twin, my_chan)

    def down_copy(k, h):
        block = total.at[k, piece(h)]
        return remote(block, block, down_s.at[k, h], down_r.at[k, h], under, my_chan)

    def gs_copy(to, at):
        return remote(gsum.at[at], gsum.at[at], gs_s.at[to], gs_r.at[at], to, my_chan)

    def forward(x):
        return (jnp.dot(fh[...], x, preferred_element_type=jnp.float32)
                + jnp.dot(fl[...], x, preferred_element_type=jnp.float32))

    def inverse(real, imag):
        both = jnp.concatenate([real, imag], axis=0)
        high = both.astype(jnp.bfloat16)
        low = (both - high.astype(jnp.float32)).astype(jnp.bfloat16)
        return (jnp.dot(ih[...], high, preferred_element_type=jnp.float32)
                + jnp.dot(ih[...], low, preferred_element_type=jnp.float32)
                + jnp.dot(il[...], high, preferred_element_type=jnp.float32))

    def column(row):
        return jnp.transpose(jnp.broadcast_to(row, (128, rows)))[:, 0:1]

    barrier = pltpu.get_barrier_semaphore()
    others(shards, me, lambda p: pl.semaphore_signal(barrier, inc=1, device_id=(p, my_chan), device_id_type=MESH))
    others(groups, my_chan, lambda p: pl.semaphore_signal(barrier, inc=1, device_id=(me, p), device_id_type=MESH))
    pl.semaphore_wait(barrier, shards + groups - 2)

    has_past, has_after = me > 0, me < shards - 1
    detours, depth = chunks - DIRECT, min(DEPTH, chunks)

    def send_cot(k):
        @pl.when(has_past)
        def _():
            cot_copy(k).start()

    def send_tok(k):
        @pl.when(has_after & ((side == 0) | (k >= detours)))
        def _():
            tok_copy(k).start()

        @pl.when(has_after & (side == 1) & (k < detours))
        def _():
            detour_copy(k).start()

    def pass_on(k):
        @pl.when((side == 0) & (level < top) & (k < detours))
        def _():
            detour_copy(k).wait_recv()
            hop_copy(k).start()

    every(depth, send_cot)

    @pl.when(me == 0)
    def _():
        htok[...] = jnp.zeros_like(htok)

    @pl.when(me == shards - 1)
    def _():
        hcot[...] = jnp.zeros_like(hcot)

    def squares(k, sums):
        v = tok[:, cols(k)].astype(jnp.float32)
        return sums + jnp.sum(v * v, axis=1, keepdims=True)

    sums = lax.fori_loop(0, chunks, squares, jnp.zeros((rows, 1), jnp.float32))
    ssq[my_chan] = jnp.transpose(jnp.broadcast_to(sums, (rows, 128)))[0:8]
    others(groups, my_chan, lambda p: ssq_copy(p, my_chan).start())

    def first(k):
        spec_h[k] = forward(fil[:, cols(k)])
        spec_g[k] = forward(cot[:, cols(k)])

    every(chunks, first)
    others(groups, my_chan, lambda p: ssq_copy(my_chan, p).wait_recv())
    fac[...] = lax.rsqrt(jnp.sum(ssq[...], axis=0) / model_width + 1e-06)
    own_fac = column(fac[0:1])

    def second(k):
        at = cols(k)
        normed = (tok[:, at].astype(jnp.float32) * own_fac * gain[:, at]).astype(jnp.bfloat16)
        nrm[k] = normed
        spec_a[k] = forward(normed)

    every(chunks, second)

    def climb(k, h):
        @pl.when((k >= 0) & (k < chunks))
        def _():
            at = piece(h)

            @pl.when(level == 0)
            def _():
                acc[k, at] = part[k, at].astype(jnp.bfloat16)

            @pl.when(level > 0)
            def _():
                up_copy(k, h).wait_recv()
                acc[k, at] = (part[k, at] + below[k, at].astype(jnp.float32)).astype(jnp.bfloat16)

            @pl.when(level < top)
            def _():
                up_copy(k, h).start()

            @pl.when(level == top)
            def _():
                near_copy(k, h).start()

    def descend(k, h):
        @pl.when((k >= 0) & (k < chunks))
        def _():
            at = piece(h)

            @pl.when(level == top)
            def _():
                near_copy(k, h).wait_recv()
                total[k, at] = (acc[k, at].astype(jnp.float32) + near[k, at].astype(jnp.float32)).astype(jnp.bfloat16)

            @pl.when(level < top)
            def _():
                down_copy(k, h).wait_recv()

            @pl.when(level > 0)
            def _():
                down_copy(k, h).start()

    def tick(i, h):
        climb(i - level, h)
        descend(i - pairs - (top - level), h)

    def backward(k):
        at = cols(k)

        @pl.when(has_past)
        def _():
            cot_copy(k).wait_send()

        @pl.when(k + depth < chunks)
        def _():
            send_cot(k + depth)

        @pl.when(k + depth >= chunks)
        def _():
            send_tok(k + depth - chunks)

        @pl.when(has_after)
        def _():
            cot_copy(k).wait_recv()
        later = forward(hcot[k])
        g_r = spec_g[k, :rows] + sign * later[rows:]
        g_i = spec_g[k, rows:] - sign * later[:rows]
        a_r, a_i = spec_a[k, :rows], spec_a[k, rows:]
        part[k] = inverse(g_r * a_r + g_i * a_i, g_i * a_r - g_r * a_i) * scale
        tick(k, 0)
        h_r, h_i = spec_h[k, :rows], spec_h[k, rows:]
        upstream = inverse(g_r * h_r + g_i * h_i, g_i * h_r - g_r * h_i)
        igrad[:, at] = upstream.astype(jnp.bfloat16)
        unit = tok[:, at].astype(jnp.float32) * own_fac
        gsum[me, :, at] = jnp.sum(upstream * unit, axis=0, keepdims=True) * scale
        tick(k, 1)

    every(chunks, backward)
    others(shards, me, lambda p: gs_copy(p, me).start())

    def onward(k):
        @pl.when(has_past)
        def _():
            tok_copy(k).wait_recv()
        before = forward(htok[k])
        x_r = spec_a[k, :rows] - sign * before[rows:]
        x_i = spec_a[k, rows:] + sign * before[:rows]
        h_r, h_i = spec_h[k, :rows], spec_h[k, rows:]
        conv[:, cols(k)] = inverse(x_r * h_r - x_i * h_i, x_r * h_i + x_i * h_r).astype(jnp.bfloat16)

    def last(k):
        @pl.when(k < chunks)
        def _():
            @pl.when(has_after)
            def _():
                tok_copy(k).wait_send()

            @pl.when(k + depth < chunks)
            def _():
                send_tok(k + depth)
            pass_on(k)
        tick(chunks + k, 0)

        @pl.when(k > 0)
        def _():
            onward(k - 1)
        tick(chunks + k, 1)

    every(chunks + 1, last)

    def rest(i):
        tick(i, 0)
        tick(i, 1)

    every(chunks + 2 * pairs - 1, rest, 2 * chunks + 1)
    others(shards, me, lambda p: gs_copy(me, p).wait_recv())
    ggrad[...] = jnp.sum(gsum[...], axis=0)

    def finish(k):
        fgrad[:, cols(k)] = total[k]

    every(chunks, finish)

    others(groups, my_chan, lambda p: ssq_copy(p, my_chan).wait_send())
    others(shards, me, lambda p: gs_copy(p, me).wait_send())

    def drained(k):
        @pl.when((side == 0) & (level < top) & (k < detours))
        def _():
            hop_copy(k).wait_send()
        for h in range(2):
            @pl.when(level < top)
            def _():
                up_copy(k, h).wait_send()

            @pl.when(level == top)
            def _():
                near_copy(k, h).wait_send()

            @pl.when(level > 0)
            def _():
                down_copy(k, h).wait_send()

    every(chunks, drained)


def local(tokens, cotangent, filters, gain):
    rows, channels = tokens.shape
    shards, groups = lax.axis_size("seq"), lax.axis_size("chan")
    width = 256 if channels % 256 == 0 else channels
    chunks = channels // width
    sizes = (shards, groups, chunks, width, channels * groups, 1.0 / math.sqrt(rows * shards))
    vmem = pl.BlockSpec(memory_space=pltpu.VMEM)
    f32, bf16 = jnp.float32, jnp.bfloat16
    dma = pltpu.SemaphoreType.DMA
    block = pltpu.VMEM((chunks, rows, width), bf16)
    conv, igrad, fgrad, ggrad = pl.pallas_call(
        functools.partial(kernel, sizes),
        out_shape=(
            jax.ShapeDtypeStruct((rows, channels), bf16),
            jax.ShapeDtypeStruct((rows, channels), bf16),
            jax.ShapeDtypeStruct((rows, channels), bf16),
            jax.ShapeDtypeStruct((1, channels), f32),
        ),
        in_specs=[vmem] * 8,
        out_specs=(vmem,) * 4,
        scratch_shapes=[
            block, block, block, block,
            pltpu.VMEM((groups, 8, rows), f32),
            pltpu.VMEM((8, rows), f32),
            pltpu.VMEM((chunks, 2 * rows, width), f32),
            pltpu.VMEM((chunks, 2 * rows, width), f32),
            pltpu.VMEM((chunks, 2 * rows, width), f32),
            pltpu.VMEM((chunks, rows, width), f32),
            block, block, block, block,
            pltpu.VMEM((shards, 1, channels), f32),
            dma((chunks,)), dma((chunks,)), dma((chunks,)), dma((chunks,)), dma((chunks,)), dma((chunks,)),
            dma((groups,)), dma((groups,)),
            dma((chunks, 2)), dma((chunks, 2)), dma((chunks, 2)), dma((chunks, 2)), dma((chunks, 2)), dma((chunks, 2)),
            dma((shards,)), dma((shards,)),
        ],
        compiler_params=pltpu.CompilerParams(
            collective_id=0, has_side_effects=True, vmem_limit_bytes=56 * 1024 * 1024),
    )(tokens, cotangent, filters, gain[None], *(jnp.asarray(m) for m in transforms(rows)))
    return conv, igrad, fgrad.astype(f32), ggrad[0]


def solution(mesh):
    placed = (P("seq", "chan"), P("seq", "chan"), P(None, "chan"), P("chan"))
    return jax.shard_map(
        local,
        mesh=mesh,
        in_specs=placed,
        out_specs=(P("seq", "chan"), P("seq", "chan"), P(None, "chan"), P("chan")),
        check_vma=False,
    )
```

```python
import functools
import math

import jax
import jax.numpy as jnp
import ml_dtypes
import numpy as np
from jax import lax
from jax.experimental import pallas as pl
from jax.experimental.pallas import tpu as pltpu
from jax.sharding import PartitionSpec as P

MESH = pl.DeviceIdType.MESH
DEPTH = 3
DIRECT = 1
GAP = 3


def halves(matrix):
    high = matrix.astype(ml_dtypes.bfloat16)
    low = (matrix - high.astype(np.float64)).astype(ml_dtypes.bfloat16)
    return high, low


def transforms(rows):
    odd = 2 * np.arange(rows)[:, None] + 1
    angle = np.pi / (2 * rows) * ((odd * np.arange(rows)[None, :]) % (4 * rows))
    forward = np.concatenate([np.cos(angle), -np.sin(angle)], axis=0)
    return (*halves(forward), *halves(forward.T / rows))


def kernel(
    sizes,
    tok, cot, fil, gain, fh, fl, ih, il,
    conv, igrad, fgrad, ggrad,
    nrm, htok, hcot, hop, ssq, fac, spec_h, spec_a, spec_g, part, below, over, acc, near, total, gsum,
    cot_s, cot_r, tok_s, tok_r, hop_s, hop_r, ssq_s, ssq_r,
    up_s, up_r, sink_s, sink_r, near_s, near_r, down_s, down_r, rise_s, rise_r, gs_s, gs_r,
):
    shards, groups, chunks, width, model_width, scale = sizes
    rows = tok.shape[0]
    half = rows // 2
    pairs = shards // 2
    me, my_chan = lax.axis_index("seq"), lax.axis_index("chan")
    side, level = lax.rem(me, 2), lax.div(me, 2)
    twin = me + 1 - 2 * side
    top = pairs - 1
    past, after = lax.rem(me + shards - 1, shards), lax.rem(me + 1, shards)
    above, under = lax.rem(me + 2, shards), lax.rem(me + shards - 2, shards)
    sign = (1 - 2 * (lax.broadcasted_iota(jnp.int32, (rows, width), 0) & 1)).astype(jnp.float32)

    def cols(k):
        return pl.ds(pl.multiple_of(k * width, width), width)

    def every(count, body, first=0):
        lax.fori_loop(first, count, lambda i, c: (body(i), c)[1], 0)

    def others(count, mine, body):
        def step(i):
            @pl.when(i != mine)
            def _():
                body(i)
        every(count, step)

    def remote(src, dst, ssem, rsem, seq, chan):
        return pltpu.make_async_remote_copy(
            src_ref=src, dst_ref=dst, send_sem=ssem, recv_sem=rsem, device_id=(seq, chan), device_id_type=MESH)

    def cot_copy(k):
        return remote(cot.at[:, cols(k)], hcot.at[k], cot_s.at[k], cot_r.at[k], past, my_chan)

    def tok_copy(k):
        return remote(nrm.at[k], htok.at[k], tok_s.at[k], tok_r.at[k], after, my_chan)

    def tok_detour(k):
        return remote(nrm.at[k], hop.at[k], tok_s.at[k], hop_r.at[k], twin, my_chan)

    def cot_detour(k):
        return remote(cot.at[:, cols(k)], hop.at[k], cot_s.at[k], hop_r.at[k], twin, my_chan)

    def tok_onward(k):
        return remote(hop.at[k], htok.at[k], hop_s.at[k], tok_r.at[k], above, my_chan)

    def cot_onward(k):
        return remote(hop.at[k], hcot.at[k], hop_s.at[k], cot_r.at[k], under, my_chan)

    def ssq_copy(to, at):
        return remote(ssq.at[at], ssq.at[at], ssq_s.at[to], ssq_r.at[at], me, to)

    def piece(h):
        return pl.ds(pl.multiple_of(h * half, half), half)

    def message(src, dst, ssem, rsem, k, h, seq):
        return remote(src.at[k, piece(h)], dst.at[k, piece(h)], ssem.at[k, h], rsem.at[k, h], seq, my_chan)

    def up_copy(k, h):
        return message(acc, below, up_s, up_r, k, h, above)

    def sink_copy(k, h):
        return message(acc, over, sink_s, sink_r, k, h, under)

    def near_copy(k, h):
        return message(acc, near, near_s, near_r, k, h, twin)

    def down_copy(k, h):
        return message(total, total, down_s, down_r, k, h, under)

    def rise_copy(k, h):
        return message(total, total, rise_s, rise_r, k, h, above)

    def gs_copy(to, at):
        return remote(gsum.at[at], gsum.at[at], gs_s.at[to], gs_r.at[at], to, my_chan)

    def forward(x):
        return (jnp.dot(fh[...], x, preferred_element_type=jnp.float32)
                + jnp.dot(fl[...], x, preferred_element_type=jnp.float32))

    def inverse(real, imag):
        both = jnp.concatenate([real, imag], axis=0)
        high = both.astype(jnp.bfloat16)
        low = (both - high.astype(jnp.float32)).astype(jnp.bfloat16)
        return (jnp.dot(ih[...], high, preferred_element_type=jnp.float32)
                + jnp.dot(ih[...], low, preferred_element_type=jnp.float32)
                + jnp.dot(il[...], high, preferred_element_type=jnp.float32))

    def column(row):
        return jnp.transpose(jnp.broadcast_to(row, (128, rows)))[:, 0:1]

    barrier = pltpu.get_barrier_semaphore()
    others(shards, me, lambda p: pl.semaphore_signal(barrier, inc=1, device_id=(p, my_chan), device_id_type=MESH))
    others(groups, my_chan, lambda p: pl.semaphore_signal(barrier, inc=1, device_id=(me, p), device_id_type=MESH))
    pl.semaphore_wait(barrier, shards + groups - 2)

    has_past, has_after = me > 0, me < shards - 1
    early, depth = chunks // 2, min(DEPTH, chunks)
    tok_turns = jnp.where(side == 0, 0, jnp.where(level < top - 1, chunks - DIRECT, jnp.where(level < top, early, 0)))
    cot_turns = jnp.where((side == 0) & (level == top), early, 0)
    tok_passes = jnp.where(side == 1, 0, jnp.where(level < top - 1, chunks - DIRECT, jnp.where(level < top, early, 0)))
    cot_passes = jnp.where((side == 1) & (level == top), early, 0)

    def send_cot(k):
        @pl.when(has_past & (k >= cot_turns))
        def _():
            cot_copy(k).start()

        @pl.when(has_past & (k < cot_turns))
        def _():
            cot_detour(k).start()

    def send_tok(k):
        @pl.when(has_after & (k >= tok_turns))
        def _():
            tok_copy(k).start()

        @pl.when(has_after & (k < tok_turns))
        def _():
            tok_detour(k).start()

    def pass_tok(k):
        @pl.when(k < tok_passes)
        def _():
            tok_detour(k).wait_recv()
            tok_onward(k).start()

    def pass_cot(k):
        @pl.when(k < cot_passes)
        def _():
            cot_detour(k).wait_recv()
            cot_onward(k).start()

    every(depth, send_cot)

    @pl.when(me == 0)
    def _():
        htok[...] = jnp.zeros_like(htok)

    @pl.when(me == shards - 1)
    def _():
        hcot[...] = jnp.zeros_like(hcot)

    def squares(k, sums):
        v = tok[:, cols(k)].astype(jnp.float32)
        return sums + jnp.sum(v * v, axis=1, keepdims=True)

    sums = lax.fori_loop(0, chunks, squares, jnp.zeros((rows, 1), jnp.float32))
    ssq[my_chan] = jnp.transpose(jnp.broadcast_to(sums, (rows, 128)))[0:8]
    others(groups, my_chan, lambda p: ssq_copy(p, my_chan).start())

    def first(k):
        spec_h[k] = forward(fil[:, cols(k)])
        spec_g[k] = forward(cot[:, cols(k)])

    for k in range(chunks):
        first(k)
    others(groups, my_chan, lambda p: ssq_copy(my_chan, p).wait_recv())
    every(min(depth, early), pass_cot)
    fac[...] = lax.rsqrt(jnp.sum(ssq[...], axis=0) / model_width + 1e-06)
    own_fac = column(fac[0:1])

    def second(k):
        at = cols(k)
        normed = (tok[:, at].astype(jnp.float32) * own_fac * gain[:, at]).astype(jnp.bfloat16)
        nrm[k] = normed
        spec_a[k] = forward(normed)

    for k in range(chunks):
        second(k)

    def climb(k, h, hub):
        at = piece(h)
        acc[k, at] = part[k, at].astype(jnp.bfloat16)

        @pl.when((level > 0) & (level <= hub))
        def _():
            up_copy(k, h).wait_recv()

        @pl.when((level < top) & (level >= hub))
        def _():
            sink_copy(k, h).wait_recv()

        @pl.when((level > 0) & (level < hub) | (level == hub) & (hub == top))
        def _():
            acc[k, at] = (part[k, at] + below[k, at].astype(jnp.float32)).astype(jnp.bfloat16)

        @pl.when((level < top) & (level > hub))
        def _():
            acc[k, at] = (part[k, at] + over[k, at].astype(jnp.float32)).astype(jnp.bfloat16)

        @pl.when((level == hub) & (hub < top))
        def _():
            arrived = below[k, at].astype(jnp.float32) + over[k, at].astype(jnp.float32)
            acc[k, at] = (part[k, at] + arrived).astype(jnp.bfloat16)

        @pl.when(level < hub)
        def _():
            up_copy(k, h).start()

        @pl.when(level > hub)
        def _():
            sink_copy(k, h).start()

        @pl.when(level == hub)
        def _():
            near_copy(k, h).start()

    def spread(k, h, hub):
        at = piece(h)

        @pl.when(level == hub)
        def _():
            near_copy(k, h).wait_recv()
            total[k, at] = (acc[k, at].astype(jnp.float32) + near[k, at].astype(jnp.float32)).astype(jnp.bfloat16)

        @pl.when(level < hub)
        def _():
            down_copy(k, h).wait_recv()

        @pl.when(level > hub)
        def _():
            rise_copy(k, h).wait_recv()

        @pl.when((level > 0) & (level <= hub))
        def _():
            down_copy(k, h).start()

        @pl.when((level < top) & (level >= hub))
        def _():
            rise_copy(k, h).start()

    classes = ((top, 0, early), (top - 1, early, chunks))

    def lags(hub):
        climbing = jnp.where(level < hub, level, jnp.where(level > hub, top - level, max(hub, top - hub)))
        return climbing * GAP, (max(hub, top - hub) + 1 + jnp.abs(level - hub)) * GAP

    def step(t, lag, begin, end, body):
        m = t - lag

        @pl.when((m >= 2 * begin) & (m < 2 * end))
        def _():
            body(lax.div(m, 2), lax.rem(m, 2))

    def tick(t):
        for hub, begin, end in classes:
            climbing, spreading = lags(hub)
            step(t, spreading, begin, end, lambda k, h: spread(k, h, hub))
            step(t, climbing, begin, end, lambda k, h: climb(k, h, hub))

    def backward(k):
        at = cols(k)

        @pl.when(has_past)
        def _():
            cot_copy(k).wait_send()

        @pl.when(k + depth < chunks)
        def _():
            send_cot(k + depth)

        @pl.when(k + depth >= chunks)
        def _():
            send_tok(k + depth - chunks)

        @pl.when(has_after)
        def _():
            cot_copy(k).wait_recv()
        later = forward(hcot[k])

        @pl.when((k + 2 >= depth) & (k + 2 < early))
        def _():
            pass_cot(k + 2)
        g_r = spec_g[k, :rows] + sign * later[rows:]
        g_i = spec_g[k, rows:] - sign * later[:rows]
        a_r, a_i = spec_a[k, :rows], spec_a[k, rows:]
        part[k] = inverse(g_r * a_r + g_i * a_i, g_i * a_r - g_r * a_i) * scale
        tick(2 * k)
        h_r, h_i = spec_h[k, :rows], spec_h[k, rows:]
        upstream = inverse(g_r * h_r + g_i * h_i, g_i * h_r - g_r * h_i)
        igrad[:, at] = upstream.astype(jnp.bfloat16)
        unit = tok[:, at].astype(jnp.float32) * own_fac
        gsum[me, :, at] = jnp.sum(upstream * unit, axis=0, keepdims=True) * scale
        tick(2 * k + 1)

    every(chunks, backward)
    others(shards, me, lambda p: gs_copy(p, me).start())

    def onward(k):
        @pl.when(has_past)
        def _():
            tok_copy(k).wait_recv()
        before = forward(htok[k])
        x_r = spec_a[k, :rows] - sign * before[rows:]
        x_i = spec_a[k, rows:] + sign * before[:rows]
        h_r, h_i = spec_h[k, :rows], spec_h[k, rows:]
        conv[:, cols(k)] = inverse(x_r * h_r - x_i * h_i, x_r * h_i + x_i * h_r).astype(jnp.bfloat16)

    def last(k):
        @pl.when(k < chunks)
        def _():
            @pl.when(has_after)
            def _():
                tok_copy(k).wait_send()

            @pl.when(k + depth < chunks)
            def _():
                send_tok(k + depth)
            pass_tok(k)
        tick(2 * (chunks + k))

        @pl.when(k > 0)
        def _():
            onward(k - 1)
        tick(2 * (chunks + k) + 1)

    every(chunks + 1, last)

    ticks = max(2 * end + GAP * (max(hub, top - hub) + 1 + max(hub, top - hub)) for hub, begin, end in classes)
    every(ticks, tick, 4 * chunks + 2)
    others(shards, me, lambda p: gs_copy(me, p).wait_recv())
    ggrad[...] = jnp.sum(gsum[...], axis=0)

    def finish(k):
        fgrad[:, cols(k)] = total[k]

    every(chunks, finish)

    others(groups, my_chan, lambda p: ssq_copy(p, my_chan).wait_send())
    others(shards, me, lambda p: gs_copy(p, me).wait_send())

    def drained(k):
        @pl.when((k < tok_passes) | (k < cot_passes))
        def _():
            tok_onward(k).wait_send()
        hub = jnp.where(k < early, top, top - 1)
        for h in range(2):
            @pl.when(level < hub)
            def _():
                up_copy(k, h).wait_send()

            @pl.when(level > hub)
            def _():
                sink_copy(k, h).wait_send()

            @pl.when(level == hub)
            def _():
                near_copy(k, h).wait_send()

            @pl.when((level > 0) & (level <= hub))
            def _():
                down_copy(k, h).wait_send()

            @pl.when((level < top) & (level >= hub))
            def _():
                rise_copy(k, h).wait_send()

    every(chunks, drained)


def local(tokens, cotangent, filters, gain):
    rows, channels = tokens.shape
    shards, groups = lax.axis_size("seq"), lax.axis_size("chan")
    width = 256 if channels % 256 == 0 else channels
    chunks = channels // width
    sizes = (shards, groups, chunks, width, channels * groups, 1.0 / math.sqrt(rows * shards))
    vmem = pl.BlockSpec(memory_space=pltpu.VMEM)
    f32, bf16 = jnp.float32, jnp.bfloat16
    dma = pltpu.SemaphoreType.DMA
    block = pltpu.VMEM((chunks, rows, width), bf16)
    conv, igrad, fgrad, ggrad = pl.pallas_call(
        functools.partial(kernel, sizes),
        out_shape=(
            jax.ShapeDtypeStruct((rows, channels), bf16),
            jax.ShapeDtypeStruct((rows, channels), bf16),
            jax.ShapeDtypeStruct((rows, channels), bf16),
            jax.ShapeDtypeStruct((1, channels), f32),
        ),
        in_specs=[vmem] * 8,
        out_specs=(vmem,) * 4,
        scratch_shapes=[
            block, block, block, block,
            pltpu.VMEM((groups, 8, rows), f32),
            pltpu.VMEM((8, rows), f32),
            pltpu.VMEM((chunks, 2 * rows, width), f32),
            pltpu.VMEM((chunks, 2 * rows, width), f32),
            pltpu.VMEM((chunks, 2 * rows, width), f32),
            pltpu.VMEM((chunks, rows, width), f32),
            block, block, block, block, block,
            pltpu.VMEM((shards, 1, channels), f32),
            dma((chunks,)), dma((chunks,)), dma((chunks,)), dma((chunks,)), dma((chunks,)), dma((chunks,)),
            dma((groups,)), dma((groups,)),
            *[dma((chunks, 2))] * 10,
            dma((shards,)), dma((shards,)),
        ],
        compiler_params=pltpu.CompilerParams(
            collective_id=0, has_side_effects=True, vmem_limit_bytes=56 * 1024 * 1024),
    )(tokens, cotangent, filters, gain[None], *(jnp.asarray(m) for m in transforms(rows)))
    return conv, igrad, fgrad.astype(f32), ggrad[0]


def solution(mesh):
    placed = (P("seq", "chan"), P("seq", "chan"), P(None, "chan"), P("chan"))
    return jax.shard_map(
        local,
        mesh=mesh,
        in_specs=placed,
        out_specs=(P("seq", "chan"), P("seq", "chan"), P(None, "chan"), P("chan")),
        check_vma=False,
    )
```

```python
import functools
import math

import jax
import jax.numpy as jnp
import ml_dtypes
import numpy as np
from jax import lax
from jax.experimental import pallas as pl
from jax.experimental.pallas import tpu as pltpu
from jax.sharding import PartitionSpec as P

MESH = pl.DeviceIdType.MESH
DEPTH = 3
GAP = 3
EARLY = 6
LAG = 2
REDUCE = 2
GATHER = 4
PARTS = 4
AHEAD = 8
DIRECT = 1


def halves(matrix):
    high = matrix.astype(ml_dtypes.bfloat16)
    low = (matrix - high.astype(np.float64)).astype(ml_dtypes.bfloat16)
    return high, low


def transforms(rows):
    odd = 2 * np.arange(rows)[:, None] + 1
    angle = np.pi / (2 * rows) * ((odd * np.arange(rows)[None, :]) % (4 * rows))
    forward = np.concatenate([np.cos(angle), -np.sin(angle)], axis=0)
    return (*halves(forward), *halves(forward.T / rows))


def kernel(
    sizes,
    tok_in, cot_in, fil_in, gain_in, fh_in, fl_in, ih_in, il_in,
    conv_hbm, igrad_hbm, total_hbm, ggrad_hbm,
    conv, igrad, total, ggrad, tok, cot, fil, gain, fh, fl, ih, il, loaded,
    nrm, htok, hcot, hop, ssq, fac, spec_h, spec_a, spec_g, part, below, acc, near, rs, mine, yours, gsum,
    cot_s, cot_r, tok_s, tok_r, hop_s, hop_r, ssq_s, ssq_r,
    up_s, up_r, near_s, near_r, down_s, down_r, rs_s, rs_r, swap_s, swap_r, ag_s, ag_r, gs_s, gs_r, out_s,
):
    shards, groups, chunks, width, model_width, scale = sizes
    rows = tok.shape[0]
    inputs = (tok_in, cot_in, fil_in, gain_in, fh_in, fl_in, ih_in, il_in)
    held = (tok, cot, fil, gain, fh, fl, ih, il)
    half = rows // 2
    pairs = shards // 2
    share, owners = rs.shape[2], rows // rs.shape[2]
    me, my_chan = lax.axis_index("seq"), lax.axis_index("chan")
    side, level = lax.rem(me, 2), lax.div(me, 2)
    twin = me + 1 - 2 * side
    top = pairs - 1
    past, after = lax.rem(me + shards - 1, shards), lax.rem(me + 1, shards)
    above, under = lax.rem(me + 2, shards), lax.rem(me + shards - 2, shards)
    sign = (1 - 2 * (lax.broadcasted_iota(jnp.int32, (rows, width), 0) & 1)).astype(jnp.float32)

    def cols(k):
        return pl.ds(pl.multiple_of(k * width, width), width)

    def every(count, body, first=0):
        lax.fori_loop(first, count, lambda i, c: (body(i), c)[1], 0)

    def others(count, mine, body):
        def step(i):
            @pl.when(i != mine)
            def _():
                body(i)
        every(count, step)

    def remote(src, dst, ssem, rsem, seq, chan):
        return pltpu.make_async_remote_copy(
            src_ref=src, dst_ref=dst, send_sem=ssem, recv_sem=rsem, device_id=(seq, chan), device_id_type=MESH)

    def cot_copy(k):
        return remote(cot_in.at[:, cols(k)], hcot.at[k], cot_s.at[k], cot_r.at[k], past, my_chan)

    def tok_copy(k):
        return remote(nrm.at[k], htok.at[k], tok_s.at[k], tok_r.at[k], after, my_chan)

    def tok_detour(k):
        return remote(nrm.at[k], hop.at[k], tok_s.at[k], hop_r.at[k], twin, my_chan)

    def tok_onward(k):
        return remote(hop.at[k], htok.at[k], hop_s.at[k], tok_r.at[k], above, my_chan)

    def ssq_copy(to, at):
        return remote(ssq.at[at], ssq.at[at], ssq_s.at[to], ssq_r.at[at], me, to)

    def piece(h):
        return pl.ds(pl.multiple_of(h * half, half), half)

    def message(src, dst, ssem, rsem, k, h, seq):
        return remote(src.at[k, piece(h)], dst.at[k, piece(h)], ssem.at[k, h], rsem.at[k, h], seq, my_chan)

    def up_copy(k, h):
        return message(acc, below, up_s, up_r, k, h, above)

    def near_copy(k, h):
        return message(acc, near, near_s, near_r, k, h, twin)

    def down_copy(k, h):
        return message(total, total, down_s, down_r, k, h, under)

    def owned(o):
        return pl.ds(pl.multiple_of(o * share, share), share)

    def rs_copy(k, to, at):
        return remote(acc.at[k, owned(to)], rs.at[k, at], rs_s.at[k, to], rs_r.at[k, at], 2 * to + side, my_chan)

    def swap_copy(k):
        return remote(mine.at[k], yours.at[k], swap_s.at[k], swap_r.at[k], twin, my_chan)

    def ag_copy(k, to, at):
        block = total.at[k, owned(at)]
        return remote(block, block, ag_s.at[k, to], ag_r.at[k, at], 2 * to + side, my_chan)

    def conv_out(k):
        return pltpu.make_async_copy(conv.at[:, cols(k)], conv_hbm.at[:, cols(k)], out_s.at[0, k])

    def igrad_out(k):
        return pltpu.make_async_copy(igrad.at[:, cols(k)], igrad_hbm.at[:, cols(k)], out_s.at[1, k])

    def total_out():
        return pltpu.make_async_copy(total, total_hbm, out_s.at[2, 0])

    def ggrad_out():
        return pltpu.make_async_copy(ggrad, ggrad_hbm, out_s.at[2, 1])

    def gs_copy(to, at):
        return remote(gsum.at[at], gsum.at[at], gs_s.at[to], gs_r.at[at], to, my_chan)

    def forward(x):
        return (jnp.dot(fh[...], x, preferred_element_type=jnp.float32)
                + jnp.dot(fl[...], x, preferred_element_type=jnp.float32))

    def inverse(real, imag):
        both = jnp.concatenate([real, imag], axis=0)
        high = both.astype(jnp.bfloat16)
        low = (both - high.astype(jnp.float32)).astype(jnp.bfloat16)
        return (jnp.dot(ih[...], high, preferred_element_type=jnp.float32)
                + jnp.dot(ih[...], low, preferred_element_type=jnp.float32)
                + jnp.dot(il[...], high, preferred_element_type=jnp.float32))

    def column(row):
        return jnp.transpose(jnp.broadcast_to(row, (128, rows)))[:, 0:1]

    barrier = pltpu.get_barrier_semaphore()
    others(shards, me, lambda p: pl.semaphore_signal(barrier, inc=1, device_id=(p, my_chan), device_id_type=MESH))
    others(groups, my_chan, lambda p: pl.semaphore_signal(barrier, inc=1, device_id=(me, p), device_id_type=MESH))
    loads = [pltpu.make_async_copy(a, b, loaded.at[i]) for i, (a, b) in enumerate(zip(inputs, held))]
    for load in loads:
        load.start()
    pl.semaphore_wait(barrier, shards + groups - 2)

    has_past, has_after = me > 0, me < shards - 1
    early, depth, lag, turns = min(EARLY, chunks), min(DEPTH, chunks), min(LAG, chunks), chunks - DIRECT
    ahead = jnp.where((side == 0) & (level == top), min(AHEAD, chunks), 0)

    def send_cot(k):
        @pl.when(has_past)
        def _():
            cot_copy(k).start()

    def send_tok(k):
        @pl.when(has_after & ((side == 0) | (k >= turns)))
        def _():
            tok_copy(k).start()

        @pl.when(has_after & (side == 1) & (k < turns))
        def _():
            tok_detour(k).start()

    def pass_tok(k):
        @pl.when((side == 0) & (level < top) & (k < turns))
        def _():
            tok_detour(k).wait_recv()
            tok_onward(k).start()

    every(depth, send_cot)

    @pl.when(me == 0)
    def _():
        htok[...] = jnp.zeros_like(htok)

    @pl.when(me == shards - 1)
    def _():
        hcot[...] = jnp.zeros_like(hcot)

    for load in loads:
        load.wait()

    def squares(k, sums):
        v = tok[:, cols(k)].astype(jnp.float32)
        return sums + jnp.sum(v * v, axis=1, keepdims=True)

    sums = lax.fori_loop(0, chunks, squares, jnp.zeros((rows, 1), jnp.float32))
    ssq[my_chan] = jnp.transpose(jnp.broadcast_to(sums, (rows, 128)))[0:8]
    others(groups, my_chan, lambda p: ssq_copy(p, my_chan).start())

    def first(k):
        spec_h[k] = forward(fil[:, cols(k)])
        spec_g[k] = forward(cot[:, cols(k)])

    for k in range(chunks):
        first(k)
    others(groups, my_chan, lambda p: ssq_copy(my_chan, p).wait_recv())
    fac[...] = lax.rsqrt(jnp.sum(ssq[...], axis=0) / model_width + 1e-06)
    own_fac = column(fac[0:1])

    def second(k):
        at = cols(k)
        normed = (tok[:, at].astype(jnp.float32) * own_fac * gain[:, at]).astype(jnp.bfloat16)
        nrm[k] = normed
        spec_a[k] = forward(normed)

    for k in range(chunks):
        second(k)

    def climb(k, h):
        at = piece(h)

        @pl.when(level == 0)
        def _():
            acc[k, at] = part[k, at].astype(jnp.bfloat16)

        @pl.when(level > 0)
        def _():
            up_copy(k, h).wait_recv()
            acc[k, at] = (part[k, at] + below[k, at].astype(jnp.float32)).astype(jnp.bfloat16)

        @pl.when(level < top)
        def _():
            up_copy(k, h).start()

        @pl.when(level == top)
        def _():
            near_copy(k, h).start()

    def spread(k, h):
        at = piece(h)

        @pl.when(level == top)
        def _():
            near_copy(k, h).wait_recv()
            total[k, at] = (acc[k, at].astype(jnp.float32) + near[k, at].astype(jnp.float32)).astype(jnp.bfloat16)

        @pl.when(level < top)
        def _():
            down_copy(k, h).wait_recv()

        @pl.when(level > 0)
        def _():
            down_copy(k, h).start()

    def step(m, body):
        @pl.when((m >= 0) & (m < 2 * early))
        def _():
            body(lax.div(m, 2), lax.rem(m, 2))

    def tick(t):
        step(t - GAP * (top + 1 + top - level), spread)
        step(t - GAP * level, climb)

    def scatter(k):
        acc[k] = part[k].astype(jnp.bfloat16)
        others(owners, level, lambda o: rs_copy(k, o, level).start())

    def reduce(k):
        @pl.when(level < owners)
        def _():
            others(pairs, level, lambda p: rs_copy(k, level, p).wait_recv())
            rs[k, level] = acc[k, owned(level)]
            summed = lax.fori_loop(
                0, pairs, lambda p, sums: sums + rs[k, p].astype(jnp.float32), jnp.zeros((share, width), jnp.float32))
            mine[k] = summed.astype(jnp.bfloat16)
            swap_copy(k).start()

    def gather(k):
        @pl.when(level < owners)
        def _():
            swap_copy(k).wait_recv()
            total[k, owned(level)] = (mine[k].astype(jnp.float32) + yours[k].astype(jnp.float32)).astype(jnp.bfloat16)
            others(pairs, level, lambda p: ag_copy(k, p, level).start())

    def direct(i):
        for late, body in ((GATHER, gather), (REDUCE, reduce)):
            k = i - late

            @pl.when((k >= early) & (k < chunks))
            def _():
                body(k)

    def backward(k):
        at = cols(k)

        @pl.when(has_past)
        def _():
            cot_copy(k).wait_send()

        @pl.when(k + depth < chunks)
        def _():
            send_cot(k + depth)

        @pl.when((k + depth >= chunks) & (k + depth - chunks >= ahead))
        def _():
            send_tok(k + depth - chunks)

        @pl.when(k < ahead)
        def _():
            send_tok(k)

        @pl.when(has_after)
        def _():
            cot_copy(k).wait_recv()
        later = forward(hcot[k])
        g_r = spec_g[k, :rows] + sign * later[rows:]
        g_i = spec_g[k, rows:] - sign * later[:rows]
        a_r, a_i = spec_a[k, :rows], spec_a[k, rows:]
        part[k] = inverse(g_r * a_r + g_i * a_i, g_i * a_r - g_r * a_i) * scale
        tick(2 * k)

        @pl.when(k >= early)
        def _():
            scatter(k)
        h_r, h_i = spec_h[k, :rows], spec_h[k, rows:]
        upstream = inverse(g_r * h_r + g_i * h_i, g_i * h_r - g_r * h_i)
        igrad[:, at] = upstream.astype(jnp.bfloat16)
        igrad_out(k).start()
        unit = tok[:, at].astype(jnp.float32) * own_fac
        gsum[me, :, at] = jnp.sum(upstream * unit, axis=0, keepdims=True) * scale
        tick(2 * k + 1)
        direct(k)

    every(chunks, backward)
    others(shards, me, lambda p: gs_copy(p, me).start())

    def onward(k):
        @pl.when(has_past)
        def _():
            tok_copy(k).wait_recv()
        before = forward(htok[k])
        x_r = spec_a[k, :rows] - sign * before[rows:]
        x_i = spec_a[k, rows:] + sign * before[:rows]
        h_r, h_i = spec_h[k, :rows], spec_h[k, rows:]
        conv[:, cols(k)] = inverse(x_r * h_r - x_i * h_i, x_r * h_i + x_i * h_r).astype(jnp.bfloat16)
        conv_out(k).start()

    def last(k):
        @pl.when(k < chunks)
        def _():
            @pl.when(has_after)
            def _():
                tok_copy(k).wait_send()

            @pl.when((k + depth < chunks) & (k + depth >= ahead))
            def _():
                send_tok(k + depth)
            pass_tok(k)
        tick(2 * (chunks + k))

        @pl.when(k >= lag)
        def _():
            onward(k - lag)
        tick(2 * (chunks + k) + 1)
        direct(chunks + k)

    every(chunks + lag, last)

    def rest(i):
        tick(2 * i)
        tick(2 * i + 1)
        direct(i)

    every(max(early + GAP * (2 * top + 1), chunks + GATHER), rest, 2 * chunks + lag)

    def finish(k):
        others(owners, level, lambda o: ag_copy(k, level, o).wait_recv())

    every(chunks, finish, early)
    total_out().start()
    others(shards, me, lambda p: gs_copy(me, p).wait_recv())
    ggrad[...] = jnp.sum(gsum[...], axis=0)
    ggrad_out().start()

    others(groups, my_chan, lambda p: ssq_copy(p, my_chan).wait_send())
    others(shards, me, lambda p: gs_copy(p, me).wait_send())

    def drained(k):
        igrad_out(k).wait()
        conv_out(k).wait()

        @pl.when((side == 0) & (level < top) & (k < turns))
        def _():
            tok_onward(k).wait_send()

        @pl.when(k < early)
        def _():
            for h in range(2):
                @pl.when(level < top)
                def _():
                    up_copy(k, h).wait_send()

                @pl.when(level == top)
                def _():
                    near_copy(k, h).wait_send()

                @pl.when(level > 0)
                def _():
                    down_copy(k, h).wait_send()

        @pl.when(k >= early)
        def _():
            others(owners, level, lambda o: rs_copy(k, o, level).wait_send())

            @pl.when(level < owners)
            def _():
                swap_copy(k).wait_send()
                others(pairs, level, lambda p: ag_copy(k, p, level).wait_send())

    every(chunks, drained)
    total_out().wait()
    ggrad_out().wait()


def hand_over(chunks, width, conv, igrad, sums, ggrad, conv_out, igrad_out, fgrad_out, ggrad_out, narrow, wide, kept, row, sent):
    strip = conv.shape[0] // PARTS
    routes = [(ggrad, row, ggrad_out)]
    for i in range(PARTS):
        at = pl.ds(i * strip, strip)
        routes += [(a.at[at], kept.at[j, at], b.at[at]) for j, (a, b) in enumerate(((conv, conv_out), (igrad, igrad_out)))]
    loads = [pltpu.make_async_copy(sums.at[k], narrow.at[k], sent.at[0, k]) for k in range(chunks)]
    enters = [pltpu.make_async_copy(a, held, sent.at[1, i]) for i, (a, held, b) in enumerate(routes)]
    leaves = [pltpu.make_async_copy(held, b, sent.at[2, i]) for i, (a, held, b) in enumerate(routes)]
    for copy in loads + enters:
        copy.start()
    for k in range(chunks):
        at = pl.ds(k * width, width)
        loads[k].wait()
        wide[:, at] = narrow[k].astype(jnp.float32)
        leaves.append(pltpu.make_async_copy(wide.at[:, at], fgrad_out.at[:, at], sent.at[3, k]))
        leaves[-1].start()
    for enter, leave in zip(enters, leaves):
        enter.wait()
        leave.start()
    for copy in leaves:
        copy.wait()


def local(tokens, cotangent, filters, gain):
    rows, channels = tokens.shape
    shards, groups = lax.axis_size("seq"), lax.axis_size("chan")
    width = 256 if channels % 256 == 0 else channels
    chunks = channels // width
    sizes = (shards, groups, chunks, width, channels * groups, 1.0 / math.sqrt(rows * shards))
    whole = pl.BlockSpec(memory_space=pl.ANY)
    pairs = shards // 2
    share = max(16, rows // pairs)
    owners = rows // share
    f32, bf16 = jnp.float32, jnp.bfloat16
    dma = pltpu.SemaphoreType.DMA
    block = pltpu.VMEM((chunks, rows, width), bf16)
    operands = (tokens, cotangent, filters, gain[None], *(jnp.asarray(m) for m in transforms(rows)))
    conv, igrad, fgrad, ggrad = pl.pallas_call(
        functools.partial(kernel, sizes),
        out_shape=(
            jax.ShapeDtypeStruct((rows, channels), bf16),
            jax.ShapeDtypeStruct((rows, channels), bf16),
            jax.ShapeDtypeStruct((chunks, rows, width), bf16),
            jax.ShapeDtypeStruct((1, channels), f32),
        ),
        in_specs=[pl.BlockSpec(memory_space=pltpu.HBM)] * 8,
        out_specs=(whole,) * 4,
        scratch_shapes=[
            pltpu.VMEM((rows, channels), bf16), pltpu.VMEM((rows, channels), bf16), block, pltpu.VMEM((1, channels), f32),
            *[pltpu.VMEM(a.shape, a.dtype) for a in operands], dma((len(operands),)),
            block, block, block, block,
            pltpu.VMEM((groups, 8, rows), f32),
            pltpu.VMEM((8, rows), f32),
            pltpu.VMEM((chunks, 2 * rows, width), f32),
            pltpu.VMEM((chunks, 2 * rows, width), f32),
            pltpu.VMEM((chunks, 2 * rows, width), f32),
            pltpu.VMEM((chunks, rows, width), f32),
            block, block, block,
            pltpu.VMEM((chunks, pairs, share, width), bf16),
            pltpu.VMEM((chunks, share, width), bf16), pltpu.VMEM((chunks, share, width), bf16),
            pltpu.VMEM((shards, 1, channels), f32),
            dma((chunks,)), dma((chunks,)), dma((chunks,)), dma((chunks,)), dma((chunks,)), dma((chunks,)),
            dma((groups,)), dma((groups,)),
            *[dma((chunks, 2))] * 6,
            dma((chunks, owners)), dma((chunks, pairs)), dma((chunks,)), dma((chunks,)), dma((chunks, pairs)), dma((chunks, owners)),
            dma((shards,)), dma((shards,)), dma((3, max(chunks, 2))),
        ],
        compiler_params=pltpu.CompilerParams(
            collective_id=0, has_side_effects=True, vmem_limit_bytes=56 * 1024 * 1024),
    )(*operands)
    conv, igrad, fgrad, ggrad = pl.pallas_call(
        functools.partial(hand_over, chunks, width),
        out_shape=(
            jax.ShapeDtypeStruct((rows, channels), bf16),
            jax.ShapeDtypeStruct((rows, channels), bf16),
            jax.ShapeDtypeStruct((rows, channels), f32),
            jax.ShapeDtypeStruct((1, channels), f32),
        ),
        in_specs=[whole] * 4,
        out_specs=(whole,) * 4,
        scratch_shapes=[
            block, pltpu.VMEM((rows, channels), f32), pltpu.VMEM((2, rows, channels), bf16), pltpu.VMEM((1, channels), f32),
            dma((4, max(chunks, 2 * PARTS + 1)))],
        compiler_params=pltpu.CompilerParams(vmem_limit_bytes=56 * 1024 * 1024),
    )(conv, igrad, fgrad, ggrad)
    return conv, igrad, fgrad, ggrad[0]


def solution(mesh):
    placed = (P("seq", "chan"), P("seq", "chan"), P(None, "chan"), P("chan"))
    return jax.shard_map(
        local,
        mesh=mesh,
        in_specs=placed,
        out_specs=(P("seq", "chan"), P("seq", "chan"), P(None, "chan"), P("chan")),
        check_vma=False,
    )
```

```python
import functools
import math

import jax
import jax.numpy as jnp
import ml_dtypes
import numpy as np
from jax import lax
from jax.experimental import pallas as pl
from jax.experimental.pallas import tpu as pltpu
from jax.sharding import PartitionSpec as P

MESH = pl.DeviceIdType.MESH
DEPTH = 3
GAP = 3
EARLY = 7
LAG = 2
REDUCE = 2
GATHER = 4
PARTS = 4
AHEAD = 4
DIRECT = 1
CROSS = 5


def halves(matrix):
    high = matrix.astype(ml_dtypes.bfloat16)
    low = (matrix - high.astype(np.float64)).astype(ml_dtypes.bfloat16)
    return high, low


def transforms(rows):
    odd = 2 * np.arange(rows)[:, None] + 1
    angle = np.pi / (2 * rows) * ((odd * np.arange(rows)[None, :]) % (4 * rows))
    forward = np.concatenate([np.cos(angle), -np.sin(angle)], axis=0)
    return (*halves(forward), *halves(forward.T / rows))


def kernel(
    sizes,
    tok_in, cot_in, fil_in, gain_in, fh_in, fl_in, ih_in, il_in,
    conv_hbm, igrad_hbm, total_hbm, ggrad_hbm,
    conv, igrad, total, ggrad, tok, cot, fil, gain, fh, fl, ih, il, loaded,
    nrm, htok, hcot, hop, ssq, fac, spec_h, spec_a, spec_g, part, below, acc, near, rs, mine, yours, gsum,
    cot_s, cot_r, tok_s, tok_r, hop_s, hop_r, ssq_s, ssq_r,
    up_s, up_r, near_s, near_r, down_s, down_r, rs_s, rs_r, swap_s, swap_r, ag_s, ag_r, gs_s, gs_r, out_s,
):
    shards, groups, chunks, width, model_width, scale = sizes
    rows = tok.shape[0]
    inputs = (tok_in, cot_in, fil_in, gain_in, fh_in, fl_in, ih_in, il_in)
    held = (tok, cot, fil, gain, fh, fl, ih, il)
    half = rows // 2
    pairs = shards // 2
    share, owners = rs.shape[2], rows // rs.shape[2]
    me, my_chan = lax.axis_index("seq"), lax.axis_index("chan")
    side, level = lax.rem(me, 2), lax.div(me, 2)
    twin = me + 1 - 2 * side
    top = pairs - 1
    past, after = lax.rem(me + shards - 1, shards), lax.rem(me + 1, shards)
    above, under = lax.rem(me + 2, shards), lax.rem(me + shards - 2, shards)
    sign = (1 - 2 * (lax.broadcasted_iota(jnp.int32, (rows, width), 0) & 1)).astype(jnp.float32)

    def cols(k):
        return pl.ds(pl.multiple_of(k * width, width), width)

    def every(count, body, first=0):
        lax.fori_loop(first, count, lambda i, c: (body(i), c)[1], 0)

    def others(count, mine, body):
        def step(i):
            @pl.when(i != mine)
            def _():
                body(i)
        every(count, step)

    def remote(src, dst, ssem, rsem, seq, chan):
        return pltpu.make_async_remote_copy(
            src_ref=src, dst_ref=dst, send_sem=ssem, recv_sem=rsem, device_id=(seq, chan), device_id_type=MESH)

    def cot_copy(k):
        return remote(cot_in.at[:, cols(k)], hcot.at[k], cot_s.at[k], cot_r.at[k], past, my_chan)

    def tok_copy(k):
        return remote(nrm.at[k], htok.at[k], tok_s.at[k], tok_r.at[k], after, my_chan)

    def tok_detour(k):
        return remote(nrm.at[k], hop.at[k], tok_s.at[k], hop_r.at[k], twin, my_chan)

    def tok_onward(k):
        return remote(hop.at[k], htok.at[k], hop_s.at[k], tok_r.at[k], above, my_chan)

    def ssq_copy(to, at):
        return remote(ssq.at[at], ssq.at[at], ssq_s.at[to], ssq_r.at[at], me, to)

    def piece(h):
        return pl.ds(pl.multiple_of(h * half, half), half)

    def message(src, dst, ssem, rsem, k, h, seq):
        return remote(src.at[k, piece(h)], dst.at[k, piece(h)], ssem.at[k, h], rsem.at[k, h], seq, my_chan)

    def up_copy(k, h):
        return message(acc, below, up_s, up_r, k, h, above)

    def near_copy(k, h):
        return message(acc, near, near_s, near_r, k, h, twin)

    def down_copy(k, h):
        return message(total, total, down_s, down_r, k, h, under)

    def owned(o):
        return pl.ds(pl.multiple_of(o * share, share), share)

    def rs_copy(k, to, at):
        return remote(acc.at[k, owned(to)], rs.at[k, at], rs_s.at[k, to], rs_r.at[k, at], 2 * to + side, my_chan)

    def swap_copy(k):
        return remote(mine.at[k], yours.at[k], swap_s.at[k], swap_r.at[k], twin, my_chan)

    def ag_copy(k, to, at):
        block = total.at[k, owned(at)]
        return remote(block, block, ag_s.at[k, to], ag_r.at[k, at], 2 * to + side, my_chan)

    def conv_out(k):
        return pltpu.make_async_copy(conv.at[:, cols(k)], conv_hbm.at[:, cols(k)], out_s.at[0, k])

    def igrad_out(k):
        return pltpu.make_async_copy(igrad.at[:, cols(k)], igrad_hbm.at[:, cols(k)], out_s.at[1, k])

    def total_out():
        return pltpu.make_async_copy(total, total_hbm, out_s.at[2, 0])

    def ggrad_out():
        return pltpu.make_async_copy(ggrad, ggrad_hbm, out_s.at[2, 1])

    def gs_copy(to, at):
        return remote(gsum.at[at], gsum.at[at], gs_s.at[to], gs_r.at[at], to, my_chan)

    def forward(x):
        return (jnp.dot(fh[...], x, preferred_element_type=jnp.float32)
                + jnp.dot(fl[...], x, preferred_element_type=jnp.float32))

    def inverse(real, imag):
        both = jnp.concatenate([real, imag], axis=0)
        high = both.astype(jnp.bfloat16)
        low = (both - high.astype(jnp.float32)).astype(jnp.bfloat16)
        return (jnp.dot(ih[...], high, preferred_element_type=jnp.float32)
                + jnp.dot(ih[...], low, preferred_element_type=jnp.float32)
                + jnp.dot(il[...], high, preferred_element_type=jnp.float32))

    def column(row):
        return jnp.transpose(jnp.broadcast_to(row, (128, rows)))[:, 0:1]

    barrier = pltpu.get_barrier_semaphore()
    others(shards, me, lambda p: pl.semaphore_signal(barrier, inc=1, device_id=(p, my_chan), device_id_type=MESH))
    others(groups, my_chan, lambda p: pl.semaphore_signal(barrier, inc=1, device_id=(me, p), device_id_type=MESH))
    loads = [pltpu.make_async_copy(a, b, loaded.at[i]) for i, (a, b) in enumerate(zip(inputs, held))]
    for load in loads:
        load.start()
    pl.semaphore_wait(barrier, shards + groups - 2)

    has_past, has_after = me > 0, me < shards - 1
    early, depth, lag, turns = min(EARLY, chunks), min(DEPTH, chunks), min(LAG, chunks), chunks - DIRECT
    ahead = jnp.where((side == 0) & (level == top), min(AHEAD, chunks), 0)

    def send_cot(k):
        @pl.when(has_past)
        def _():
            cot_copy(k).start()

    def send_tok(k):
        @pl.when(has_after & ((side == 0) | (k >= turns)))
        def _():
            tok_copy(k).start()

        @pl.when(has_after & (side == 1) & (k < turns))
        def _():
            tok_detour(k).start()

    def pass_tok(k):
        @pl.when((side == 0) & (level < top) & (k < turns))
        def _():
            tok_detour(k).wait_recv()
            tok_onward(k).start()

    every(depth, send_cot)

    @pl.when(me == 0)
    def _():
        htok[...] = jnp.zeros_like(htok)

    @pl.when(me == shards - 1)
    def _():
        hcot[...] = jnp.zeros_like(hcot)

    for load in loads:
        load.wait()

    def squares(k, sums):
        v = tok[:, cols(k)].astype(jnp.float32)
        return sums + jnp.sum(v * v, axis=1, keepdims=True)

    sums = lax.fori_loop(0, chunks, squares, jnp.zeros((rows, 1), jnp.float32))
    ssq[my_chan] = jnp.transpose(jnp.broadcast_to(sums, (rows, 128)))[0:8]
    others(groups, my_chan, lambda p: ssq_copy(p, my_chan).start())

    def first(k):
        spec_h[k] = forward(fil[:, cols(k)])
        spec_g[k] = forward(cot[:, cols(k)])

    for k in range(chunks):
        first(k)
    others(groups, my_chan, lambda p: ssq_copy(my_chan, p).wait_recv())
    fac[...] = lax.rsqrt(jnp.sum(ssq[...], axis=0) / model_width + 1e-06)
    own_fac = column(fac[0:1])

    def second(k):
        at = cols(k)
        normed = (tok[:, at].astype(jnp.float32) * own_fac * gain[:, at]).astype(jnp.bfloat16)
        nrm[k] = normed
        spec_a[k] = forward(normed)

    for k in range(chunks):
        second(k)

    def climb(k, h):
        at = piece(h)

        @pl.when(level == 0)
        def _():
            acc[k, at] = part[k, at].astype(jnp.bfloat16)

        @pl.when(level > 0)
        def _():
            up_copy(k, h).wait_recv()
            acc[k, at] = (part[k, at] + below[k, at].astype(jnp.float32)).astype(jnp.bfloat16)

        @pl.when(level < top)
        def _():
            up_copy(k, h).start()

        @pl.when(level == top)
        def _():
            near_copy(k, h).start()

    def spread(k, h):
        at = piece(h)

        @pl.when(level == top)
        def _():
            near_copy(k, h).wait_recv()
            total[k, at] = (acc[k, at].astype(jnp.float32) + near[k, at].astype(jnp.float32)).astype(jnp.bfloat16)

        @pl.when(level < top)
        def _():
            down_copy(k, h).wait_recv()

        @pl.when(level > 0)
        def _():
            down_copy(k, h).start()

    def step(m, body):
        @pl.when((m >= 0) & (m < 2 * early))
        def _():
            body(lax.div(m, 2), lax.rem(m, 2))

    def tick(t):
        step(t - GAP * (top + top - level) - CROSS, spread)
        step(t - GAP * level, climb)

    def scatter(k):
        acc[k] = part[k].astype(jnp.bfloat16)
        others(owners, level, lambda o: rs_copy(k, o, level).start())

    def reduce(k):
        @pl.when(level < owners)
        def _():
            others(pairs, level, lambda p: rs_copy(k, level, p).wait_recv())
            rs[k, level] = acc[k, owned(level)]
            summed = lax.fori_loop(
                0, pairs, lambda p, sums: sums + rs[k, p].astype(jnp.float32), jnp.zeros((share, width), jnp.float32))
            mine[k] = summed.astype(jnp.bfloat16)
            swap_copy(k).start()

    def gather(k):
        @pl.when(level < owners)
        def _():
            swap_copy(k).wait_recv()
            total[k, owned(level)] = (mine[k].astype(jnp.float32) + yours[k].astype(jnp.float32)).astype(jnp.bfloat16)
            others(pairs, level, lambda p: ag_copy(k, p, level).start())

    def direct(i):
        for late, body in ((GATHER, gather), (REDUCE, reduce)):
            k = i - late

            @pl.when((k >= early) & (k < chunks))
            def _():
                body(k)

    def backward(k):
        at = cols(k)

        @pl.when(has_past)
        def _():
            cot_copy(k).wait_send()

        @pl.when(k + depth < chunks)
        def _():
            send_cot(k + depth)

        @pl.when((k + depth >= chunks) & (k + depth - chunks >= ahead))
        def _():
            send_tok(k + depth - chunks)

        @pl.when(k < ahead)
        def _():
            send_tok(k)

        @pl.when(has_after)
        def _():
            cot_copy(k).wait_recv()
        later = forward(hcot[k])
        g_r = spec_g[k, :rows] + sign * later[rows:]
        g_i = spec_g[k, rows:] - sign * later[:rows]
        a_r, a_i = spec_a[k, :rows], spec_a[k, rows:]
        part[k] = inverse(g_r * a_r + g_i * a_i, g_i * a_r - g_r * a_i) * scale
        tick(2 * k)

        @pl.when(k >= early)
        def _():
            scatter(k)
        h_r, h_i = spec_h[k, :rows], spec_h[k, rows:]
        upstream = inverse(g_r * h_r + g_i * h_i, g_i * h_r - g_r * h_i)
        igrad[:, at] = upstream.astype(jnp.bfloat16)
        igrad_out(k).start()
        unit = tok[:, at].astype(jnp.float32) * own_fac
        gsum[me, :, at] = jnp.sum(upstream * unit, axis=0, keepdims=True) * scale
        tick(2 * k + 1)
        direct(k)

    every(chunks, backward)
    others(shards, me, lambda p: gs_copy(p, me).start())

    def onward(k):
        @pl.when(has_past)
        def _():
            tok_copy(k).wait_recv()
        before = forward(htok[k])
        x_r = spec_a[k, :rows] - sign * before[rows:]
        x_i = spec_a[k, rows:] + sign * before[:rows]
        h_r, h_i = spec_h[k, :rows], spec_h[k, rows:]
        conv[:, cols(k)] = inverse(x_r * h_r - x_i * h_i, x_r * h_i + x_i * h_r).astype(jnp.bfloat16)
        conv_out(k).start()

    def last(k):
        @pl.when(k < chunks)
        def _():
            @pl.when(has_after)
            def _():
                tok_copy(k).wait_send()

            @pl.when((k + depth < chunks) & (k + depth >= ahead))
            def _():
                send_tok(k + depth)
            pass_tok(k)
        tick(2 * (chunks + k))

        @pl.when(k >= lag)
        def _():
            onward(k - lag)
        tick(2 * (chunks + k) + 1)
        direct(chunks + k)

    every(chunks + lag, last)

    def rest(i):
        tick(2 * i)
        tick(2 * i + 1)
        direct(i)

    every(max(early + GAP * 2 * top + CROSS, chunks + GATHER), rest, 2 * chunks + lag)

    def finish(k):
        others(owners, level, lambda o: ag_copy(k, level, o).wait_recv())

    every(chunks, finish, early)
    total_out().start()
    others(shards, me, lambda p: gs_copy(me, p).wait_recv())
    ggrad[...] = jnp.sum(gsum[...], axis=0)
    ggrad_out().start()

    others(groups, my_chan, lambda p: ssq_copy(p, my_chan).wait_send())
    others(shards, me, lambda p: gs_copy(p, me).wait_send())

    def drained(k):
        igrad_out(k).wait()
        conv_out(k).wait()

        @pl.when((side == 0) & (level < top) & (k < turns))
        def _():
            tok_onward(k).wait_send()

        @pl.when(k < early)
        def _():
            for h in range(2):
                @pl.when(level < top)
                def _():
                    up_copy(k, h).wait_send()

                @pl.when(level == top)
                def _():
                    near_copy(k, h).wait_send()

                @pl.when(level > 0)
                def _():
                    down_copy(k, h).wait_send()

        @pl.when(k >= early)
        def _():
            others(owners, level, lambda o: rs_copy(k, o, level).wait_send())

            @pl.when(level < owners)
            def _():
                swap_copy(k).wait_send()
                others(pairs, level, lambda p: ag_copy(k, p, level).wait_send())

    every(chunks, drained)
    total_out().wait()
    ggrad_out().wait()


def hand_over(chunks, width, conv, igrad, sums, ggrad, conv_out, igrad_out, fgrad_out, ggrad_out, narrow, wide, kept, row, sent):
    strip = conv.shape[0] // PARTS
    routes = [(ggrad, row, ggrad_out)]
    for i in range(PARTS):
        at = pl.ds(i * strip, strip)
        routes += [(a.at[at], kept.at[j, at], b.at[at]) for j, (a, b) in enumerate(((conv, conv_out), (igrad, igrad_out)))]
    loads = [pltpu.make_async_copy(sums.at[k], narrow.at[k], sent.at[0, k]) for k in range(chunks)]
    enters = [pltpu.make_async_copy(a, held, sent.at[1, i]) for i, (a, held, b) in enumerate(routes)]
    leaves = [pltpu.make_async_copy(held, b, sent.at[2, i]) for i, (a, held, b) in enumerate(routes)]
    for copy in loads + enters:
        copy.start()
    for k in range(chunks):
        at = pl.ds(k * width, width)
        loads[k].wait()
        wide[:, at] = narrow[k].astype(jnp.float32)
        leaves.append(pltpu.make_async_copy(wide.at[:, at], fgrad_out.at[:, at], sent.at[3, k]))
        leaves[-1].start()
    for enter, leave in zip(enters, leaves):
        enter.wait()
        leave.start()
    for copy in leaves:
        copy.wait()


def local(tokens, cotangent, filters, gain):
    rows, channels = tokens.shape
    shards, groups = lax.axis_size("seq"), lax.axis_size("chan")
    width = 256 if channels % 256 == 0 else channels
    chunks = channels // width
    sizes = (shards, groups, chunks, width, channels * groups, 1.0 / math.sqrt(rows * shards))
    whole = pl.BlockSpec(memory_space=pl.ANY)
    pairs = shards // 2
    share = max(16, rows // pairs)
    owners = rows // share
    f32, bf16 = jnp.float32, jnp.bfloat16
    dma = pltpu.SemaphoreType.DMA
    block = pltpu.VMEM((chunks, rows, width), bf16)
    operands = (tokens, cotangent, filters, gain[None], *(jnp.asarray(m) for m in transforms(rows)))
    conv, igrad, fgrad, ggrad = pl.pallas_call(
        functools.partial(kernel, sizes),
        out_shape=(
            jax.ShapeDtypeStruct((rows, channels), bf16),
            jax.ShapeDtypeStruct((rows, channels), bf16),
            jax.ShapeDtypeStruct((chunks, rows, width), bf16),
            jax.ShapeDtypeStruct((1, channels), f32),
        ),
        in_specs=[pl.BlockSpec(memory_space=pltpu.HBM)] * 8,
        out_specs=(whole,) * 4,
        scratch_shapes=[
            pltpu.VMEM((rows, channels), bf16), pltpu.VMEM((rows, channels), bf16), block, pltpu.VMEM((1, channels), f32),
            *[pltpu.VMEM(a.shape, a.dtype) for a in operands], dma((len(operands),)),
            block, block, block, block,
            pltpu.VMEM((groups, 8, rows), f32),
            pltpu.VMEM((8, rows), f32),
            pltpu.VMEM((chunks, 2 * rows, width), f32),
            pltpu.VMEM((chunks, 2 * rows, width), f32),
            pltpu.VMEM((chunks, 2 * rows, width), f32),
            pltpu.VMEM((chunks, rows, width), f32),
            block, block, block,
            pltpu.VMEM((chunks, pairs, share, width), bf16),
            pltpu.VMEM((chunks, share, width), bf16), pltpu.VMEM((chunks, share, width), bf16),
            pltpu.VMEM((shards, 1, channels), f32),
            dma((chunks,)), dma((chunks,)), dma((chunks,)), dma((chunks,)), dma((chunks,)), dma((chunks,)),
            dma((groups,)), dma((groups,)),
            *[dma((chunks, 2))] * 6,
            dma((chunks, owners)), dma((chunks, pairs)), dma((chunks,)), dma((chunks,)), dma((chunks, pairs)), dma((chunks, owners)),
            dma((shards,)), dma((shards,)), dma((3, max(chunks, 2))),
        ],
        compiler_params=pltpu.CompilerParams(
            collective_id=0, has_side_effects=True, vmem_limit_bytes=56 * 1024 * 1024),
    )(*operands)
    conv, igrad, fgrad, ggrad = pl.pallas_call(
        functools.partial(hand_over, chunks, width),
        out_shape=(
            jax.ShapeDtypeStruct((rows, channels), bf16),
            jax.ShapeDtypeStruct((rows, channels), bf16),
            jax.ShapeDtypeStruct((rows, channels), f32),
            jax.ShapeDtypeStruct((1, channels), f32),
        ),
        in_specs=[whole] * 4,
        out_specs=(whole,) * 4,
        scratch_shapes=[
            block, pltpu.VMEM((rows, channels), f32), pltpu.VMEM((2, rows, channels), bf16), pltpu.VMEM((1, channels), f32),
            dma((4, max(chunks, 2 * PARTS + 1)))],
        compiler_params=pltpu.CompilerParams(vmem_limit_bytes=56 * 1024 * 1024),
    )(conv, igrad, fgrad, ggrad)
    return conv, igrad, fgrad, ggrad[0]


def solution(mesh):
    placed = (P("seq", "chan"), P("seq", "chan"), P(None, "chan"), P("chan"))
    return jax.shard_map(
        local,
        mesh=mesh,
        in_specs=placed,
        out_specs=(P("seq", "chan"), P("seq", "chan"), P(None, "chan"), P("chan")),
        check_vma=False,
    )
```

```python
import functools
import math

import jax
import jax.numpy as jnp
import ml_dtypes
import numpy as np
from jax import lax
from jax.experimental import pallas as pl
from jax.experimental.pallas import tpu as pltpu
from jax.sharding import PartitionSpec as P

MESH = pl.DeviceIdType.MESH
DEPTH = 3
GAP = 3
EARLY = 7
LAG = 2
REDUCE = 2
GATHER = 4
PARTS = 4
AHEAD = 4
DIRECT = 1
CROSS = 5


def halves(matrix):
    high = matrix.astype(ml_dtypes.bfloat16)
    low = (matrix - high.astype(np.float64)).astype(ml_dtypes.bfloat16)
    return high, low


def transforms(rows):
    odd = 2 * np.arange(rows)[:, None] + 1
    angle = np.pi / (2 * rows) * ((odd * np.arange(rows)[None, :]) % (4 * rows))
    forward = np.concatenate([np.cos(angle), -np.sin(angle)], axis=0)
    return (*halves(forward), *halves(forward.T / rows))


def kernel(
    sizes,
    tok_in, cot_in, fil_in, gain_in, fh_in, fl_in, ih_in, il_in,
    conv_hbm, igrad_hbm, total_hbm, ggrad_hbm,
    conv, igrad, total, ggrad, tok, cot, fil, gain, fh, fl, ih, il, loaded,
    nrm, htok, hcot, hop, ssq, fac, spec_h, spec_a, spec_g, part, below, acc, near, rs, mine, yours, gsum,
    cot_s, cot_r, tok_s, tok_r, hop_s, hop_r, ssq_s, ssq_r,
    up_s, up_r, near_s, near_r, down_s, down_r, rs_s, rs_r, swap_s, swap_r, ag_s, ag_r, gs_s, gs_r, out_s,
):
    shards, groups, chunks, width, model_width, scale = sizes
    rows = tok.shape[0]
    inputs = (tok_in, cot_in, fil_in, gain_in, fh_in, fl_in, ih_in, il_in)
    held = (tok, cot, fil, gain, fh, fl, ih, il)
    half = rows // 2
    pairs = shards // 2
    share, owners = rs.shape[2], rows // rs.shape[2]
    me, my_chan = lax.axis_index("seq"), lax.axis_index("chan")
    side, level = lax.rem(me, 2), lax.div(me, 2)
    twin = me + 1 - 2 * side
    top = pairs - 1
    past, after = lax.rem(me + shards - 1, shards), lax.rem(me + 1, shards)
    above, under = lax.rem(me + 2, shards), lax.rem(me + shards - 2, shards)
    sign = (1 - 2 * (lax.broadcasted_iota(jnp.int32, (rows, width), 0) & 1)).astype(jnp.float32)

    def cols(k):
        return pl.ds(pl.multiple_of(k * width, width), width)

    def every(count, body, first=0):
        lax.fori_loop(first, count, lambda i, c: (body(i), c)[1], 0)

    def others(count, mine, body):
        def step(i):
            @pl.when(i != mine)
            def _():
                body(i)
        every(count, step)

    def remote(src, dst, ssem, rsem, seq, chan):
        return pltpu.make_async_remote_copy(
            src_ref=src, dst_ref=dst, send_sem=ssem, recv_sem=rsem, device_id=(seq, chan), device_id_type=MESH)

    def cot_copy(k):
        return remote(cot_in.at[:, cols(k)], hcot.at[k], cot_s.at[k], cot_r.at[k], past, my_chan)

    def tok_copy(k):
        return remote(nrm.at[k], htok.at[k], tok_s.at[k], tok_r.at[k], after, my_chan)

    def tok_detour(k):
        return remote(nrm.at[k], hop.at[k], tok_s.at[k], hop_r.at[k], twin, my_chan)

    def tok_onward(k):
        return remote(hop.at[k], htok.at[k], hop_s.at[k], tok_r.at[k], above, my_chan)

    def ssq_copy(to, at):
        return remote(ssq.at[at], ssq.at[at], ssq_s.at[to], ssq_r.at[at], me, to)

    def piece(h):
        return pl.ds(pl.multiple_of(h * half, half), half)

    def message(src, dst, ssem, rsem, k, h, seq):
        return remote(src.at[k, piece(h)], dst.at[k, piece(h)], ssem.at[k, h], rsem.at[k, h], seq, my_chan)

    def up_copy(k, h):
        return message(acc, below, up_s, up_r, k, h, above)

    def near_copy(k, h):
        return message(acc, near, near_s, near_r, k, h, twin)

    def down_copy(k, h):
        return message(total, total, down_s, down_r, k, h, under)

    def owned(o):
        return pl.ds(pl.multiple_of(o * share, share), share)

    def rs_copy(k, to, at):
        return remote(acc.at[k, owned(to)], rs.at[k, at], rs_s.at[k, to], rs_r.at[k, at], 2 * to + side, my_chan)

    def swap_copy(k):
        return remote(mine.at[k], yours.at[k], swap_s.at[k], swap_r.at[k], twin, my_chan)

    def ag_copy(k, to, at):
        block = total.at[k, owned(at)]
        return remote(block, block, ag_s.at[k, to], ag_r.at[k, at], 2 * to + side, my_chan)

    def conv_out(k):
        return pltpu.make_async_copy(conv.at[:, cols(k)], conv_hbm.at[:, cols(k)], out_s.at[0, k])

    def igrad_out(k):
        return pltpu.make_async_copy(igrad.at[:, cols(k)], igrad_hbm.at[:, cols(k)], out_s.at[1, k])

    def total_out(k):
        return pltpu.make_async_copy(total.at[k], total_hbm.at[k], out_s.at[2, k])

    def ggrad_out():
        return pltpu.make_async_copy(ggrad, ggrad_hbm, out_s.at[3, 0])

    def gs_copy(to, at):
        return remote(gsum.at[at], gsum.at[at], gs_s.at[to], gs_r.at[at], to, my_chan)

    def forward(x):
        return (jnp.dot(fh[...], x, preferred_element_type=jnp.float32)
                + jnp.dot(fl[...], x, preferred_element_type=jnp.float32))

    def inverse(real, imag):
        both = jnp.concatenate([real, imag], axis=0)
        high = both.astype(jnp.bfloat16)
        low = (both - high.astype(jnp.float32)).astype(jnp.bfloat16)
        return (jnp.dot(ih[...], high, preferred_element_type=jnp.float32)
                + jnp.dot(ih[...], low, preferred_element_type=jnp.float32)
                + jnp.dot(il[...], high, preferred_element_type=jnp.float32))

    def column(row):
        return jnp.transpose(jnp.broadcast_to(row, (128, rows)))[:, 0:1]

    barrier = pltpu.get_barrier_semaphore()
    others(shards, me, lambda p: pl.semaphore_signal(barrier, inc=1, device_id=(p, my_chan), device_id_type=MESH))
    others(groups, my_chan, lambda p: pl.semaphore_signal(barrier, inc=1, device_id=(me, p), device_id_type=MESH))
    loads = [pltpu.make_async_copy(a, b, loaded.at[i]) for i, (a, b) in enumerate(zip(inputs, held))]
    for load in loads:
        load.start()
    pl.semaphore_wait(barrier, shards + groups - 2)

    has_past, has_after = me > 0, me < shards - 1
    early, depth, lag, turns = min(EARLY, chunks), min(DEPTH, chunks), min(LAG, chunks), chunks - DIRECT
    ahead = jnp.where((side == 0) & (level == top), min(AHEAD, chunks), 0)

    def send_cot(k):
        @pl.when(has_past)
        def _():
            cot_copy(k).start()

    def send_tok(k):
        @pl.when(has_after & ((side == 0) | (k >= turns)))
        def _():
            tok_copy(k).start()

        @pl.when(has_after & (side == 1) & (k < turns))
        def _():
            tok_detour(k).start()

    def pass_tok(k):
        @pl.when((side == 0) & (level < top) & (k < turns))
        def _():
            tok_detour(k).wait_recv()
            tok_onward(k).start()

    every(depth, send_cot)

    @pl.when(me == 0)
    def _():
        htok[...] = jnp.zeros_like(htok)

    @pl.when(me == shards - 1)
    def _():
        hcot[...] = jnp.zeros_like(hcot)

    for load in loads:
        load.wait()

    def squares(k, sums):
        v = tok[:, cols(k)].astype(jnp.float32)
        return sums + jnp.sum(v * v, axis=1, keepdims=True)

    sums = lax.fori_loop(0, chunks, squares, jnp.zeros((rows, 1), jnp.float32))
    ssq[my_chan] = jnp.transpose(jnp.broadcast_to(sums, (rows, 128)))[0:8]
    others(groups, my_chan, lambda p: ssq_copy(p, my_chan).start())

    def first(k):
        spec_h[k] = forward(fil[:, cols(k)])
        spec_g[k] = forward(cot[:, cols(k)])

    for k in range(chunks):
        first(k)
    others(groups, my_chan, lambda p: ssq_copy(my_chan, p).wait_recv())
    fac[...] = lax.rsqrt(jnp.sum(ssq[...], axis=0) / model_width + 1e-06)
    own_fac = column(fac[0:1])

    def second(k):
        at = cols(k)
        normed = (tok[:, at].astype(jnp.float32) * own_fac * gain[:, at]).astype(jnp.bfloat16)
        nrm[k] = normed
        spec_a[k] = forward(normed)

    for k in range(chunks):
        second(k)

    def climb(k, h):
        at = piece(h)

        @pl.when(level == 0)
        def _():
            acc[k, at] = part[k, at].astype(jnp.bfloat16)

        @pl.when(level > 0)
        def _():
            up_copy(k, h).wait_recv()
            acc[k, at] = (part[k, at] + below[k, at].astype(jnp.float32)).astype(jnp.bfloat16)

        @pl.when(level < top)
        def _():
            up_copy(k, h).start()

        @pl.when(level == top)
        def _():
            near_copy(k, h).start()

    def spread(k, h):
        at = piece(h)

        @pl.when(level == top)
        def _():
            near_copy(k, h).wait_recv()
            total[k, at] = (acc[k, at].astype(jnp.float32) + near[k, at].astype(jnp.float32)).astype(jnp.bfloat16)

        @pl.when(level < top)
        def _():
            down_copy(k, h).wait_recv()

        @pl.when(level > 0)
        def _():
            down_copy(k, h).start()

        @pl.when(h == 1)
        def _():
            total_out(k).start()

    def step(m, body):
        @pl.when((m >= 0) & (m < 2 * early))
        def _():
            body(lax.div(m, 2), lax.rem(m, 2))

    def tick(t):
        step(t - GAP * (top + top - level) - CROSS, spread)
        step(t - GAP * level, climb)

    def scatter(k):
        acc[k] = part[k].astype(jnp.bfloat16)
        others(owners, level, lambda o: rs_copy(k, o, level).start())

    def reduce(k):
        @pl.when(level < owners)
        def _():
            others(pairs, level, lambda p: rs_copy(k, level, p).wait_recv())
            rs[k, level] = acc[k, owned(level)]
            summed = lax.fori_loop(
                0, pairs, lambda p, sums: sums + rs[k, p].astype(jnp.float32), jnp.zeros((share, width), jnp.float32))
            mine[k] = summed.astype(jnp.bfloat16)
            swap_copy(k).start()

    def gather(k):
        @pl.when(level < owners)
        def _():
            swap_copy(k).wait_recv()
            total[k, owned(level)] = (mine[k].astype(jnp.float32) + yours[k].astype(jnp.float32)).astype(jnp.bfloat16)
            others(pairs, level, lambda p: ag_copy(k, p, level).start())

    def direct(i):
        for late, body in ((GATHER, gather), (REDUCE, reduce)):
            k = i - late

            @pl.when((k >= early) & (k < chunks))
            def _():
                body(k)

    def backward(k):
        at = cols(k)

        @pl.when(has_past)
        def _():
            cot_copy(k).wait_send()

        @pl.when(k + depth < chunks)
        def _():
            send_cot(k + depth)

        @pl.when((k + depth >= chunks) & (k + depth - chunks >= ahead))
        def _():
            send_tok(k + depth - chunks)

        @pl.when(k < ahead)
        def _():
            send_tok(k)

        @pl.when(has_after)
        def _():
            cot_copy(k).wait_recv()
        later = forward(hcot[k])
        g_r = spec_g[k, :rows] + sign * later[rows:]
        g_i = spec_g[k, rows:] - sign * later[:rows]
        a_r, a_i = spec_a[k, :rows], spec_a[k, rows:]
        part[k] = inverse(g_r * a_r + g_i * a_i, g_i * a_r - g_r * a_i) * scale
        tick(2 * k)

        @pl.when(k >= early)
        def _():
            scatter(k)
        h_r, h_i = spec_h[k, :rows], spec_h[k, rows:]
        upstream = inverse(g_r * h_r + g_i * h_i, g_i * h_r - g_r * h_i)
        igrad[:, at] = upstream.astype(jnp.bfloat16)
        igrad_out(k).start()
        unit = tok[:, at].astype(jnp.float32) * own_fac
        gsum[me, :, at] = jnp.sum(upstream * unit, axis=0, keepdims=True) * scale
        tick(2 * k + 1)
        direct(k)

    every(chunks, backward)
    others(shards, me, lambda p: gs_copy(p, me).start())

    def onward(k):
        @pl.when(has_past)
        def _():
            tok_copy(k).wait_recv()
        before = forward(htok[k])
        x_r = spec_a[k, :rows] - sign * before[rows:]
        x_i = spec_a[k, rows:] + sign * before[:rows]
        h_r, h_i = spec_h[k, :rows], spec_h[k, rows:]
        conv[:, cols(k)] = inverse(x_r * h_r - x_i * h_i, x_r * h_i + x_i * h_r).astype(jnp.bfloat16)
        conv_out(k).start()

    def last(k):
        @pl.when(k < chunks)
        def _():
            @pl.when(has_after)
            def _():
                tok_copy(k).wait_send()

            @pl.when((k + depth < chunks) & (k + depth >= ahead))
            def _():
                send_tok(k + depth)
            pass_tok(k)
        tick(2 * (chunks + k))

        @pl.when(k >= lag)
        def _():
            onward(k - lag)
        tick(2 * (chunks + k) + 1)
        direct(chunks + k)

    every(chunks + lag, last)

    def rest(i):
        tick(2 * i)
        tick(2 * i + 1)
        direct(i)

    every(max(early + GAP * 2 * top + CROSS, chunks + GATHER), rest, 2 * chunks + lag)

    def finish(k):
        others(owners, level, lambda o: ag_copy(k, level, o).wait_recv())
        total_out(k).start()

    every(chunks, finish, early)
    others(shards, me, lambda p: gs_copy(me, p).wait_recv())
    ggrad[...] = jnp.sum(gsum[...], axis=0)
    ggrad_out().start()

    others(groups, my_chan, lambda p: ssq_copy(p, my_chan).wait_send())
    others(shards, me, lambda p: gs_copy(p, me).wait_send())

    def drained(k):
        igrad_out(k).wait()
        total_out(k).wait()
        conv_out(k).wait()

        @pl.when((side == 0) & (level < top) & (k < turns))
        def _():
            tok_onward(k).wait_send()

        @pl.when(k < early)
        def _():
            for h in range(2):
                @pl.when(level < top)
                def _():
                    up_copy(k, h).wait_send()

                @pl.when(level == top)
                def _():
                    near_copy(k, h).wait_send()

                @pl.when(level > 0)
                def _():
                    down_copy(k, h).wait_send()

        @pl.when(k >= early)
        def _():
            others(owners, level, lambda o: rs_copy(k, o, level).wait_send())

            @pl.when(level < owners)
            def _():
                swap_copy(k).wait_send()
                others(pairs, level, lambda p: ag_copy(k, p, level).wait_send())

    every(chunks, drained)
    ggrad_out().wait()


def hand_over(chunks, width, conv, igrad, sums, ggrad, conv_out, igrad_out, fgrad_out, ggrad_out, narrow, wide, kept, row, sent):
    strip = conv.shape[0] // PARTS
    routes = [(ggrad, row, ggrad_out)]
    for i in range(PARTS):
        at = pl.ds(i * strip, strip)
        routes += [(a.at[at], kept.at[j, at], b.at[at]) for j, (a, b) in enumerate(((conv, conv_out), (igrad, igrad_out)))]
    loads = [pltpu.make_async_copy(sums.at[k], narrow.at[k], sent.at[0, k]) for k in range(chunks)]
    enters = [pltpu.make_async_copy(a, held, sent.at[1, i]) for i, (a, held, b) in enumerate(routes)]
    leaves = [pltpu.make_async_copy(held, b, sent.at[2, i]) for i, (a, held, b) in enumerate(routes)]
    for copy in loads + enters:
        copy.start()
    for k in range(chunks):
        at = pl.ds(k * width, width)
        loads[k].wait()
        wide[:, at] = narrow[k].astype(jnp.float32)
        leaves.append(pltpu.make_async_copy(wide.at[:, at], fgrad_out.at[:, at], sent.at[3, k]))
        leaves[-1].start()
    for enter, leave in zip(enters, leaves):
        enter.wait()
        leave.start()
    for copy in leaves:
        copy.wait()


def local(tokens, cotangent, filters, gain):
    rows, channels = tokens.shape
    shards, groups = lax.axis_size("seq"), lax.axis_size("chan")
    width = 256 if channels % 256 == 0 else channels
    chunks = channels // width
    sizes = (shards, groups, chunks, width, channels * groups, 1.0 / math.sqrt(rows * shards))
    whole = pl.BlockSpec(memory_space=pl.ANY)
    pairs = shards // 2
    share = max(16, rows // pairs)
    owners = rows // share
    f32, bf16 = jnp.float32, jnp.bfloat16
    dma = pltpu.SemaphoreType.DMA
    block = pltpu.VMEM((chunks, rows, width), bf16)
    operands = (tokens, cotangent, filters, gain[None], *(jnp.asarray(m) for m in transforms(rows)))
    conv, igrad, fgrad, ggrad = pl.pallas_call(
        functools.partial(kernel, sizes),
        out_shape=(
            jax.ShapeDtypeStruct((rows, channels), bf16),
            jax.ShapeDtypeStruct((rows, channels), bf16),
            jax.ShapeDtypeStruct((chunks, rows, width), bf16),
            jax.ShapeDtypeStruct((1, channels), f32),
        ),
        in_specs=[pl.BlockSpec(memory_space=pltpu.HBM)] * 8,
        out_specs=(whole,) * 4,
        scratch_shapes=[
            pltpu.VMEM((rows, channels), bf16), pltpu.VMEM((rows, channels), bf16), block, pltpu.VMEM((1, channels), f32),
            *[pltpu.VMEM(a.shape, a.dtype) for a in operands], dma((len(operands),)),
            block, block, block, block,
            pltpu.VMEM((groups, 8, rows), f32),
            pltpu.VMEM((8, rows), f32),
            pltpu.VMEM((chunks, 2 * rows, width), f32),
            pltpu.VMEM((chunks, 2 * rows, width), f32),
            pltpu.VMEM((chunks, 2 * rows, width), f32),
            pltpu.VMEM((chunks, rows, width), f32),
            block, block, block,
            pltpu.VMEM((chunks, pairs, share, width), bf16),
            pltpu.VMEM((chunks, share, width), bf16), pltpu.VMEM((chunks, share, width), bf16),
            pltpu.VMEM((shards, 1, channels), f32),
            dma((chunks,)), dma((chunks,)), dma((chunks,)), dma((chunks,)), dma((chunks,)), dma((chunks,)),
            dma((groups,)), dma((groups,)),
            *[dma((chunks, 2))] * 6,
            dma((chunks, owners)), dma((chunks, pairs)), dma((chunks,)), dma((chunks,)), dma((chunks, pairs)), dma((chunks, owners)),
            dma((shards,)), dma((shards,)), dma((4, chunks)),
        ],
        compiler_params=pltpu.CompilerParams(
            collective_id=0, has_side_effects=True, vmem_limit_bytes=56 * 1024 * 1024),
    )(*operands)
    conv, igrad, fgrad, ggrad = pl.pallas_call(
        functools.partial(hand_over, chunks, width),
        out_shape=(
            jax.ShapeDtypeStruct((rows, channels), bf16),
            jax.ShapeDtypeStruct((rows, channels), bf16),
            jax.ShapeDtypeStruct((rows, channels), f32),
            jax.ShapeDtypeStruct((1, channels), f32),
        ),
        in_specs=[whole] * 4,
        out_specs=(whole,) * 4,
        scratch_shapes=[
            block, pltpu.VMEM((rows, channels), f32), pltpu.VMEM((2, rows, channels), bf16), pltpu.VMEM((1, channels), f32),
            dma((4, max(chunks, 2 * PARTS + 1)))],
        compiler_params=pltpu.CompilerParams(vmem_limit_bytes=56 * 1024 * 1024),
    )(conv, igrad, fgrad, ggrad)
    return conv, igrad, fgrad, ggrad[0]


def solution(mesh):
    placed = (P("seq", "chan"), P("seq", "chan"), P(None, "chan"), P("chan"))
    return jax.shard_map(
        local,
        mesh=mesh,
        in_specs=placed,
        out_specs=(P("seq", "chan"), P("seq", "chan"), P(None, "chan"), P("chan")),
        check_vma=False,
    )
```
